256 devices in a mesh: grp: 32 (over x_lo, z, core), blk: 8 (over x_hi, y).
Axes of the slice: x: 4 (x_hi: 2, x_lo: 2; x = x_hi * 2 + x_lo), y: 4, z: 8, core: 2. Of those that a mesh axis runs over, the one named last changes fastest.
Arguments:
- walker_matrix: float32 [32, 8, 1024, 1024], P('grp', 'blk'), may hold values from -6 to 6
- updates: bfloat16 [32, 8, 4, 1024, 256], P('grp', 'blk'), may hold values from -0.19921875 to 0.19921875
- update_rows: int32 [32, 8, 4, 256], P('grp', 'blk'), may hold values from 0 to 1023, as said below
- left_table: float32 [1024, 256], replicated, may hold values from -0.1875 to 0.1875
- right_table: float32 [1024, 256], replicated, may hold values from -0.1875 to 0.1875
- assignment: int32 [8, 32], P('blk'), may hold values from 0 to 31, each once within a row
- momentum_sum: int32 [16, 16], replicated, may hold values from 0 to 15, as said below
- transfer_momentum: int32 [32], replicated, may hold values from 0 to 15
- transfer_frequency: int32 [32], replicated, may hold values from 0 to 15
- ownership: int32 [32], P('blk'), may hold values from 0 to 31, each once
- g4_prior: float32 [32, 32, 256, 256], P('grp', 'blk'), may hold values from -6 to 6
Outputs:
- g4_slices: float32 [32, 32, 256, 256], P('grp', 'blk')
The draws below stay inside these ranges and needn't reach their ends.
Inputs may be any that keep to these rules, and one draw needn't show every extreme that they name: `update_rows`: within each update of each walker the 256 row indices are distinct. `assignment`: each row is a permutation of the grp indices. `momentum_sum`: the addition table of a periodic 4 x 4 cluster under a relabeling of its momenta; every row and column is a permutation. `ownership`: a permutation of the transfer slots.
All inputs are finite; a program needn't handle non-finite values.
Results may differ from the reference program's by a relative error of at most 0.0003.
Values sent between devices are 32-bit elements; how exact they have to be, the bound alone decides.
No kernel may reach another device: no remote copies, remote signals or barrier semaphores. Data moves between devices by JAX's collectives and lax.ppermute only.
A program may use at most 128 MiB of HBM per device.

```python
import jax
import jax.numpy as jnp
from jax import lax

ORDER = 1024
RANK = 256
UPD = 4
CL = 4
NW = 16
NK = 16
KW = 256
Q = 32
N_GRP = 32
N_BLK = 8


def draw_update_rows(key, part):
    keys = jax.random.split(jax.random.fold_in(key, 11), N_GRP * N_BLK * UPD)
    drawn = jax.vmap(lambda one_key: jax.random.permutation(one_key, ORDER)[:RANK])(keys)
    return drawn.reshape(N_GRP, N_BLK, UPD, RANK).astype(jnp.int32)


def draw_momentum_sum(key, part):
    relabel = jax.random.permutation(jax.random.fold_in(key, 17), NK).astype(jnp.int32)
    inverse = jnp.zeros((NK,), jnp.int32).at[relabel].set(jnp.arange(NK, dtype=jnp.int32))
    first = inverse[:, None]
    second = inverse[None, :]
    combined = (first // CL + second // CL) % CL * CL + (first % CL + second % CL) % CL
    return relabel[combined].astype(jnp.int32)


def with_ends(values, own_key, least, largest):
    longest = values.shape.index(max(values.shape))
    spots = []
    for shift in (0, 1):
        where = [jax.random.randint(jax.random.fold_in(own_key, axis), (), 0, length) for axis, length in enumerate(values.shape)]
        where[longest] = (where[longest] + shift) % values.shape[longest]
        spots.append(tuple(where))
    return values.at[spots[0]].set(least).at[spots[1]].set(largest)


def level_of(rng, dims, shards, smallest, largest):
    def one(dim, shards_of):
        heights = jax.random.uniform(jax.random.fold_in(jax.random.fold_in(rng, 6), dim), (shards_of,), jnp.float32, smallest / len(shards), largest / len(shards))
        return jnp.repeat(jnp.exp(heights), dims[dim] // shards_of).reshape((-1,) + (1,) * (len(dims) - dim - 1))

    loudness = one(*shards[0])
    for cut in shards[1:]:
        loudness = loudness * one(*cut)
    return loudness


def noise(key, dims, scale, bound, cuts=(), kind=jnp.bfloat16):
    loudness = level_of(key, dims, cuts, -0.22, 0.18) if cuts else 1.0
    entries = jax.random.normal(key, dims, jnp.float32) * scale * loudness
    return jnp.minimum(jnp.maximum(entries, -bound), bound).astype(kind)


def setup_inputs(seed: int = 0) -> dict:
    arg_keys = jax.random.split(jax.random.key(seed), 12)
    return {
        "walker_matrix": noise(arg_keys[0], (N_GRP, N_BLK, ORDER, ORDER), 1.0, 6.0, ((0, 32), (1, 8)), jnp.float32),
        "updates": noise(arg_keys[1], (N_GRP, N_BLK, UPD, ORDER, RANK), 0.03125, 0.19921875, ((0, 32), (1, 8))),
        "update_rows": draw_update_rows(jax.random.fold_in(arg_keys[11], 71), 0),
        "left_table": noise(arg_keys[3], (ORDER, KW), ORDER ** -0.5, 0.1875, (), jnp.float32),
        "right_table": noise(arg_keys[4], (ORDER, KW), ORDER ** -0.5, 0.1875, (), jnp.float32),
        "assignment": jax.vmap(lambda own: jax.random.permutation(own, N_GRP))(jax.random.split(arg_keys[5], N_BLK)).reshape((N_BLK, N_GRP)).astype(jnp.int32),
        "momentum_sum": draw_momentum_sum(jax.random.fold_in(arg_keys[11], 71), 0),
        "transfer_momentum": with_ends(jax.random.randint(arg_keys[7], (Q,), 0, NK), jax.random.fold_in(arg_keys[7], 1), 0, NK - 1).astype(jnp.int32),
        "transfer_frequency": with_ends(jax.random.randint(arg_keys[8], (Q,), 0, NW), jax.random.fold_in(arg_keys[8], 1), 0, NW - 1).astype(jnp.int32),
        "ownership": jax.random.permutation(arg_keys[9], Q).astype(jnp.int32),
        "g4_prior": noise(arg_keys[10], (N_GRP, Q, KW, KW), 1.0, 6.0, ((0, 32), (1, 8)), jnp.float32),
    }


highest = lax.Precision.HIGHEST


def measure_walker(matrix, updates_here, rows_here, left_table, right_table):
    for number in range(UPD):
        picked = matrix[rows_here[number]]
        matrix = matrix + jnp.dot(updates_here[number].astype(jnp.float32), picked, precision=highest)
    partial_value = jnp.dot(matrix, right_table, precision=highest)
    return jnp.dot(left_table.T, partial_value, precision=highest)


def shift_rows(momentum_sum, moment_ids, freq_ids):
    labels = jnp.arange(KW, dtype=jnp.int32)
    momenta = labels // NW
    frequency = labels % NW
    return momentum_sum[momenta[None, :], moment_ids[:, None]] * NW + (frequency[None, :] + freq_ids[:, None]) % NW


def cycle_terms(greens_cycle, shifted):
    flipped = jnp.swapaxes(greens_cycle, 1, 2)

    def one_transfer(row_ids):
        picked = jnp.take(flipped, row_ids, axis=1)
        picked = jnp.take(picked, row_ids, axis=2)
        return jnp.sum(greens_cycle * picked, axis=0)

    return jax.vmap(one_transfer)(shifted)


def reference(walker_matrix, updates, update_rows, left_table, right_table, assignment, momentum_sum, transfer_momentum, transfer_frequency, ownership, g4_prior):
    walkers = N_GRP * N_BLK
    greens = lax.map(lambda walker_items: measure_walker(walker_items[0], walker_items[1], walker_items[2], left_table, right_table),
                     (walker_matrix.reshape(walkers, ORDER, ORDER), updates.reshape(walkers, UPD, ORDER, RANK), update_rows.reshape(walkers, UPD, RANK)))
    greens = greens.reshape(N_GRP, N_BLK, KW, KW)
    chosen = (assignment[:, :, None] == jnp.arange(N_GRP, dtype=jnp.int32)[None, None, :]).astype(jnp.float32)
    measured = jnp.einsum("bwa,wbij->abij", chosen, greens, precision=highest)
    shifted = shift_rows(momentum_sum, transfer_momentum[ownership], transfer_frequency[ownership])
    summed = lax.map(lambda cycle_greens: cycle_terms(cycle_greens, shifted), measured)
    return g4_prior + summed * (1.0 / N_BLK)
```

```python
import functools

import jax
import jax.numpy as jnp
from jax import lax
from jax.experimental import pallas as pl
from jax.experimental.pallas import tpu as pltpu
from jax.sharding import PartitionSpec as P

UPD = 4
RANK = 256
ORDER = 1024
NW = 16
NK = 16
KW = 256
M_CHUNKS = 8
F32 = jnp.float32
BF16 = jnp.bfloat16

ANY = pl.BlockSpec(memory_space=pl.ANY)
VMEM = pl.BlockSpec(memory_space=pltpu.VMEM)
SMEM = pl.BlockSpec(memory_space=pltpu.SMEM)


def split(x):
    hi = x.astype(BF16)
    return hi, (x - hi.astype(F32)).astype(BF16)


def mm(a, b):
    return jnp.dot(a, b, preferred_element_type=F32)


def mm_nt(a, b):
    return lax.dot_general(a, b, (((1,), (1,)), ((), ())), preferred_element_type=F32)


def walker_kernel(m_hbm, u_hbm, rows_ref, l_hbm, r_hbm, out_ref, m_v, u_v, l_v, r_v, w_ref, t_ref, sems):
    size = ORDER // M_CHUNKS
    copy_l = pltpu.make_async_copy(l_hbm, l_v, sems.at[0])
    copy_r = pltpu.make_async_copy(r_hbm, r_v, sems.at[1])
    copy_u = [pltpu.make_async_copy(u_hbm.at[u], u_v.at[u], sems.at[2 + u]) for u in range(UPD)]
    copy_m = [
        pltpu.make_async_copy(
            m_hbm.at[pl.ds(k * size, size), :], m_v.at[pl.ds(k * size, size), :], sems.at[2 + UPD + k]
        )
        for k in range(M_CHUNKS)
    ]
    copy_l.start()
    for u in reversed(range(UPD)):
        copy_u[u].start()
    for copy in copy_m:
        copy.start()
    copy_r.start()

    lane = lax.broadcasted_iota(jnp.int32, (RANK, ORDER), 1)
    copy_l.wait()
    w_ref[...] = l_v[...].T
    for u in reversed(range(UPD)):
        column = jnp.broadcast_to(rows_ref[pl.ds(u, 1), :], (128, RANK)).T[:, :1]
        chosen = jnp.where(lane == column, 1.0, 0.0).astype(BF16)
        w_hi, w_lo = split(w_ref[...])
        copy_u[u].wait()
        x = mm(w_hi, u_v[u]) + mm(w_lo, u_v[u])
        x_hi, x_lo = split(x)
        w_ref[...] += mm(x_hi, chosen) + mm(x_lo, chosen)
    w_hi, w_lo = split(w_ref[...])
    for k in range(M_CHUNKS):
        copy_m[k].wait()
        m_hi, m_lo = split(m_v[pl.ds(k * size, size), :])
        part_hi = w_hi[:, k * size : (k + 1) * size]
        part_lo = w_lo[:, k * size : (k + 1) * size]
        term = mm(part_hi, m_hi) + mm(part_lo, m_hi) + mm(part_hi, m_lo)
        if k == 0:
            t_ref[...] = term
        else:
            t_ref[...] += term
    copy_r.wait()
    t_hi, t_lo = split(t_ref[...])
    r_hi, r_lo = split(r_v[...])
    out_ref[...] = mm(t_hi, r_hi) + mm(t_lo, r_hi) + mm(t_hi, r_lo)


def walker(matrix, updates, rows, left, right):
    return pl.pallas_call(
        walker_kernel,
        out_shape=jax.ShapeDtypeStruct((KW, KW), F32),
        in_specs=[ANY, ANY, VMEM, ANY, ANY],
        out_specs=VMEM,
        scratch_shapes=[
            pltpu.VMEM((ORDER, ORDER), F32),
            pltpu.VMEM((UPD, ORDER, RANK), BF16),
            pltpu.VMEM((ORDER, KW), F32),
            pltpu.VMEM((ORDER, KW), F32),
            pltpu.VMEM((KW, ORDER), F32),
            pltpu.VMEM((KW, ORDER), F32),
            pltpu.SemaphoreType.DMA((2 + UPD + M_CHUNKS,)),
        ],
        compiler_params=pltpu.CompilerParams(vmem_limit_bytes=40 << 20),
        name="walker",
    )(matrix, updates, rows, left, right)


def route_kernel(n, targets_ref, x_ref, out_ref):
    for w in range(n):
        out_ref[targets_ref[0, w]] = x_ref[w]


def route(targets, chunks):
    return pl.pallas_call(
        functools.partial(route_kernel, chunks.shape[0]),
        out_shape=jax.ShapeDtypeStruct(chunks.shape, F32),
        in_specs=[SMEM, VMEM],
        out_specs=VMEM,
        name="route",
    )(targets, chunks)


def tail_kernel(
    scale, own_ref, ms_ref, tm_ref, tf_ref, two_ref, up_ref, down_ref, far_a_ref, far_b_ref, prior_ref, out_ref,
    pi_ref, a_ref, v_hi, v_lo,
):
    held = own_ref.shape[0]
    lanes = lax.broadcasted_iota(jnp.int32, (NW, KW), 1)
    steps = lax.broadcasted_iota(jnp.int32, (NW, KW), 0)
    for j in range(held):
        label = own_ref[j]
        moment = tm_ref[label]
        spot = (steps + tf_ref[label]) % NW
        for kappa in range(NK):
            goal = spot + ms_ref[kappa, moment] * NW
            pi_ref[pl.ds(j * KW + kappa * NW, NW), :] = jnp.where(lanes == goal, 1.0, 0.0).astype(BF16)
    half = KW // 2
    for p in range(2):
        a_ref[p] = two_ref[p]
        a_ref[2 + p] = up_ref[p]
        a_ref[4 + p] = down_ref[p]
        a_ref[6 + p, pl.ds(0, half), :] = far_a_ref[p]
        a_ref[6 + p, pl.ds(half, half), :] = far_b_ref[p]
    pi = pi_ref[...]
    for b in range(8):
        a_hi, a_lo = split(a_ref[b])
        h = mm_nt(pi, a_hi).astype(BF16)
        l = mm_nt(pi, a_lo).astype(BF16)
        for j in range(held):
            v_hi[j, pl.ds(b * KW, KW), :] = h[j * KW : (j + 1) * KW]
            v_lo[j, pl.ds(b * KW, KW), :] = l[j * KW : (j + 1) * KW]
    for j in range(held):
        pi_j = pi_ref[pl.ds(j * KW, KW), :]
        total = None
        for b in range(8):
            rows = pl.ds(b * KW, KW)
            z = mm_nt(v_hi[j, rows, :], pi_j) + mm_nt(v_lo[j, rows, :], pi_j)
            term = a_ref[b] * z
            total = term if total is None else total + term
        out_ref[j] = prior_ref[j] + total * scale


def tail(scale, ownership, momentum_sum, moments, freqs, pieces, prior):
    held = ownership.shape[0]
    return pl.pallas_call(
        functools.partial(tail_kernel, scale),
        out_shape=jax.ShapeDtypeStruct(prior.shape, F32),
        in_specs=[SMEM] * 4 + [VMEM] * 6,
        out_specs=VMEM,
        scratch_shapes=[
            pltpu.VMEM((held * KW, KW), BF16),
            pltpu.VMEM((8, KW, KW), F32),
            pltpu.VMEM((held, 8 * KW, KW), BF16),
            pltpu.VMEM((held, 8 * KW, KW), BF16),
        ],
        compiler_params=pltpu.CompilerParams(vmem_limit_bytes=48 << 20),
        name="tail",
    )(ownership, momentum_sum, moments, freqs, *pieces, prior)


def gather_cycle(own):
    half = KW // 2
    across = [(j, (j + 4) % 8) for j in range(8)]
    upward = [(j, j // 4 * 4 + (j % 4 + 1) % 4) for j in range(8)]
    downward = [(j, j // 4 * 4 + (j % 4 + 3) % 4) for j in range(8)]
    two = jnp.stack([own, lax.ppermute(own, "blk", across)])
    up = lax.ppermute(two, "blk", upward)
    down = lax.ppermute(two, "blk", downward)
    far_a = lax.ppermute(up[:, :half], "blk", upward)
    far_b = lax.ppermute(down[:, half:], "blk", downward)
    return two, up, down, far_a, far_b


def shards(
    walker_matrix, updates, update_rows, left_table, right_table, assignment, momentum_sum,
    transfer_momentum, transfer_frequency, ownership, g4_prior,
):
    n_grp = lax.axis_size("grp")
    greens = walker(walker_matrix[0, 0], updates[0, 0], update_rows[0, 0], left_table, right_table)
    chunks = lax.all_to_all(greens.reshape(n_grp, KW // n_grp, KW), "grp", 0, 0, tiled=True)
    routed = route(assignment, chunks)
    measured = lax.all_to_all(routed, "grp", 0, 0, tiled=True).reshape(KW, KW)
    pieces = gather_cycle(measured)
    scale = 1.0 / lax.axis_size("blk")
    return tail(scale, ownership, momentum_sum, transfer_momentum, transfer_frequency, pieces, g4_prior[0])[None]


def solution(mesh):
    placed = (
        P("grp", "blk", None, None),
        P("grp", "blk", None, None, None),
        P("grp", "blk", None, None),
        P(),
        P(),
        P("blk", None),
        P(),
        P(),
        P(),
        P("blk"),
        P("grp", "blk", None, None),
    )
    return jax.shard_map(
        shards, mesh=mesh, in_specs=placed, out_specs=P("grp", "blk", None, None), check_vma=False
    )
```

```python
import functools

import jax
import jax.numpy as jnp
from jax import lax
from jax.experimental import pallas as pl
from jax.experimental.pallas import tpu as pltpu
from jax.sharding import PartitionSpec as P

UPD = 4
RANK = 256
ORDER = 1024
NW = 16
NK = 16
KW = 256
M_CHUNKS = 8
F32 = jnp.float32
BF16 = jnp.bfloat16

HBM = pl.BlockSpec(memory_space=pltpu.HBM)
VMEM = pl.BlockSpec(memory_space=pltpu.VMEM)
SMEM = pl.BlockSpec(memory_space=pltpu.SMEM)


def split(x):
    hi = x.astype(BF16)
    return hi, (x - hi.astype(F32)).astype(BF16)


def mm(a, b):
    return jnp.dot(a, b, preferred_element_type=F32)


def mm_nt(a, b):
    return lax.dot_general(a, b, (((1,), (1,)), ((), ())), preferred_element_type=F32)


def walker_kernel(m_hbm, u_hbm, rows_hbm, l_hbm, r_hbm, out_ref, m_v, u_v, rows_v, l_v, r_v, w_ref, t_ref, sems):
    size = ORDER // M_CHUNKS
    copy_l = pltpu.make_async_copy(l_hbm, l_v, sems.at[0])
    copy_r = pltpu.make_async_copy(r_hbm, r_v, sems.at[1])
    copy_u = [pltpu.make_async_copy(u_hbm.at[u], u_v.at[u], sems.at[2 + u]) for u in range(UPD)]
    copy_m = [
        pltpu.make_async_copy(
            m_hbm.at[pl.ds(k * size, size), :], m_v.at[pl.ds(k * size, size), :], sems.at[2 + UPD + k]
        )
        for k in range(M_CHUNKS)
    ]
    copy_rows = pltpu.make_async_copy(rows_hbm, rows_v, sems.at[2 + UPD + M_CHUNKS])
    copy_l.start()
    copy_rows.start()
    for u in reversed(range(UPD)):
        copy_u[u].start()
    for copy in copy_m:
        copy.start()
    copy_r.start()

    lane = lax.broadcasted_iota(jnp.int32, (RANK, ORDER), 1)
    copy_l.wait()
    copy_rows.wait()
    w_ref[...] = l_v[...].T
    for u in reversed(range(UPD)):
        column = jnp.broadcast_to(rows_v[pl.ds(u, 1), :], (128, RANK)).T[:, :1]
        chosen = jnp.where(lane == column, 1.0, 0.0).astype(BF16)
        w_hi, w_lo = split(w_ref[...])
        copy_u[u].wait()
        x = mm(w_hi, u_v[u]) + mm(w_lo, u_v[u])
        x_hi, x_lo = split(x)
        w_ref[...] += mm(x_hi, chosen) + mm(x_lo, chosen)
    w_hi, w_lo = split(w_ref[...])
    for k in range(M_CHUNKS):
        copy_m[k].wait()
        m_hi, m_lo = split(m_v[pl.ds(k * size, size), :])
        part_hi = w_hi[:, k * size : (k + 1) * size]
        part_lo = w_lo[:, k * size : (k + 1) * size]
        term = mm(part_hi, m_hi) + mm(part_lo, m_hi) + mm(part_hi, m_lo)
        if k == 0:
            t_ref[...] = term
        else:
            t_ref[...] += term
    copy_r.wait()
    t_hi, t_lo = split(t_ref[...])
    r_hi, r_lo = split(r_v[...])
    out_ref[...] = mm(t_hi, r_hi) + mm(t_lo, r_hi) + mm(t_hi, r_lo)


def walker(matrix, updates, rows, left, right):
    return pl.pallas_call(
        walker_kernel,
        out_shape=jax.ShapeDtypeStruct((KW, KW), F32),
        in_specs=[HBM] * 5,
        out_specs=VMEM,
        scratch_shapes=[
            pltpu.VMEM((ORDER, ORDER), F32),
            pltpu.VMEM((UPD, ORDER, RANK), BF16),
            pltpu.VMEM((UPD, RANK), jnp.int32),
            pltpu.VMEM((ORDER, KW), F32),
            pltpu.VMEM((ORDER, KW), F32),
            pltpu.VMEM((KW, ORDER), F32),
            pltpu.VMEM((KW, ORDER), F32),
            pltpu.SemaphoreType.DMA((3 + UPD + M_CHUNKS,)),
        ],
        compiler_params=pltpu.CompilerParams(vmem_limit_bytes=60 << 20),
        name="walker",
    )(matrix, updates, rows, left, right)


def route_kernel(n, targets_ref, x_ref, out_ref):
    for w in range(n):
        out_ref[targets_ref[0, w]] = x_ref[w]


def route(targets, chunks):
    return pl.pallas_call(
        functools.partial(route_kernel, chunks.shape[0]),
        out_shape=jax.ShapeDtypeStruct(chunks.shape, F32),
        in_specs=[SMEM, VMEM],
        out_specs=VMEM,
        compiler_params=pltpu.CompilerParams(vmem_limit_bytes=8 << 20),
        name="route",
    )(targets, chunks)


def labels_kernel(own_ref, ms_ref, tm_ref, tf_ref, pi_ref):
    lanes = lax.broadcasted_iota(jnp.int32, (NW, KW), 1)
    steps = lax.broadcasted_iota(jnp.int32, (NW, KW), 0)
    for j in range(own_ref.shape[0]):
        label = own_ref[j]
        moment = tm_ref[label]
        spot = (steps + tf_ref[label]) % NW
        for kappa in range(NK):
            goal = spot + ms_ref[kappa, moment] * NW
            pi_ref[pl.ds(j * KW + kappa * NW, NW), :] = jnp.where(lanes == goal, 1.0, 0.0).astype(BF16)


def labels(ownership, momentum_sum, moments, freqs):
    held = ownership.shape[0]
    return pl.pallas_call(
        labels_kernel,
        out_shape=jax.ShapeDtypeStruct((held * KW, KW), BF16),
        in_specs=[SMEM] * 4,
        out_specs=VMEM,
        cost_estimate=pl.CostEstimate(flops=4_000_000, bytes_accessed=1_000_000, transcendentals=0),
        compiler_params=pltpu.CompilerParams(vmem_limit_bytes=8 << 20),
        name="labels",
    )(ownership, momentum_sum, moments, freqs)


def products_kernel(scale, picks, pi_ref, *refs):
    *piece_refs, total_ref, out_ref = refs
    held = total_ref.shape[0]
    pi = pi_ref[...]
    terms = [total_ref[j] for j in range(held)]
    for pick in picks:
        parts = [piece_refs[number][pl.ds(start, count), :] for number, start, count in pick]
        a = parts[0] if len(parts) == 1 else jnp.concatenate(parts, axis=0)
        a_hi, a_lo = split(a)
        v_hi = mm_nt(pi, a_hi).astype(BF16)
        v_lo = mm_nt(pi, a_lo).astype(BF16)
        a = a * scale
        for j in range(held):
            rows = slice(j * KW, (j + 1) * KW)
            terms[j] += a * (mm_nt(v_hi[rows], pi[rows]) + mm_nt(v_lo[rows], pi[rows]))
    for j in range(held):
        out_ref[j] = terms[j]


def products(scale, pi, picks, pieces, total, name):
    held = total.shape[0]
    count = len(picks)
    return pl.pallas_call(
        functools.partial(products_kernel, scale, picks),
        out_shape=jax.ShapeDtypeStruct(total.shape, F32),
        in_specs=[VMEM] * (2 + len(pieces)),
        out_specs=VMEM,
        cost_estimate=pl.CostEstimate(
            flops=count * held * 8 * KW**3, bytes_accessed=4 * KW * KW * (2 * held + count), transcendentals=0
        ),
        compiler_params=pltpu.CompilerParams(vmem_limit_bytes=16 << 20),
        name=name,
    )(pi, *pieces, total)


def cycle_products(scale, pi, own, prior):
    half = KW // 2
    whole = (0, KW)
    across = [(j, (j + 4) % 8) for j in range(8)]
    upward = [(j, j // 4 * 4 + (j % 4 + 1) % 4) for j in range(8)]
    downward = [(j, j // 4 * 4 + (j % 4 + 3) % 4) for j in range(8)]
    below = lax.ppermute(own, "blk", upward)
    above = lax.ppermute(own, "blk", downward)
    beside = lax.ppermute(own, "blk", across)
    total = products(scale, pi, [[(0, *whole)]], [own], prior, "products_own")
    below, above, beside, total = lax.optimization_barrier((below, above, beside, total))
    up = lax.ppermute(jnp.concatenate([beside, below[:half]]), "blk", upward)
    down = lax.ppermute(jnp.concatenate([beside, above[half:]]), "blk", downward)
    total = products(
        scale, pi, [[(number, *whole)] for number in range(3)], [below, above, beside], total, "products_near"
    )
    far_up = lax.ppermute(up[:half], "blk", upward)
    far_down = lax.ppermute(down[half:KW], "blk", downward)
    total = products(
        scale,
        pi,
        [[(0, *whole)], [(1, *whole)], [(0, KW, half), (1, KW, half)]],
        [up, down],
        total,
        "products_beside",
    )
    return products(scale, pi, [[(0, 0, half), (1, 0, half)]], [far_up, far_down], total, "products_far")


def shards(
    walker_matrix, updates, update_rows, left_table, right_table, assignment, momentum_sum,
    transfer_momentum, transfer_frequency, ownership, g4_prior,
):
    n_grp = lax.axis_size("grp")
    pi = labels(ownership, momentum_sum, transfer_momentum, transfer_frequency)
    greens = walker(walker_matrix[0, 0], updates[0, 0], update_rows[0, 0], left_table, right_table)
    chunks = lax.all_to_all(greens.reshape(n_grp, KW // n_grp, KW), "grp", 0, 0, tiled=True)
    routed = route(assignment, chunks)
    measured = lax.all_to_all(routed, "grp", 0, 0, tiled=True).reshape(KW, KW)
    scale = 1.0 / lax.axis_size("blk")
    return cycle_products(scale, pi, measured, g4_prior[0])[None]


def solution(mesh):
    placed = (
        P("grp", "blk", None, None),
        P("grp", "blk", None, None, None),
        P("grp", "blk", None, None),
        P(),
        P(),
        P("blk", None),
        P(),
        P(),
        P(),
        P("blk"),
        P("grp", "blk", None, None),
    )
    return jax.shard_map(
        shards, mesh=mesh, in_specs=placed, out_specs=P("grp", "blk", None, None), check_vma=False
    )
```

```python
import functools

import jax
import jax.numpy as jnp
from jax import lax
from jax.experimental import pallas as pl
from jax.experimental.pallas import tpu as pltpu
from jax.sharding import PartitionSpec as P

UPD = 4
RANK = 256
ORDER = 1024
NW = 16
NK = 16
KW = 256
M_CHUNKS = 2
F32 = jnp.float32
BF16 = jnp.bfloat16

HBM = pl.BlockSpec(memory_space=pltpu.HBM)
VMEM = pl.BlockSpec(memory_space=pltpu.VMEM)
SMEM = pl.BlockSpec(memory_space=pltpu.SMEM)


def split(x):
    hi = x.astype(BF16)
    return hi, (x - hi.astype(F32)).astype(BF16)


def mm(a, b):
    return jnp.dot(a, b, preferred_element_type=F32)


def mm_nt(a, b):
    return lax.dot_general(a, b, (((1,), (1,)), ((), ())), preferred_element_type=F32)


def mm_split(hi, lo, b):
    count = hi.shape[0]
    both = mm(jnp.concatenate([hi, lo]), b)
    return both[:count] + both[count:]


def walker_kernel(m_hbm, u_hbm, rows_hbm, l_hbm, r_hbm, out_ref, m_v, u_v, rows_v, l_v, r_v, p_ref, s_ref, sems):
    size = ORDER // M_CHUNKS
    copy_rows = pltpu.make_async_copy(rows_hbm, rows_v, sems.at[0])
    copy_l = pltpu.make_async_copy(l_hbm, l_v, sems.at[1])
    copy_r = pltpu.make_async_copy(r_hbm, r_v, sems.at[2])
    copy_u = [pltpu.make_async_copy(u_hbm.at[u], u_v.at[u], sems.at[3 + u]) for u in range(UPD)]
    copy_m = [
        pltpu.make_async_copy(
            m_hbm.at[pl.ds(k * size, size), :], m_v.at[pl.ds(k * size, size), :], sems.at[3 + UPD + k]
        )
        for k in range(M_CHUNKS)
    ]
    for copy in (copy_rows, copy_r, *copy_m, copy_l, copy_u[3], copy_u[0], copy_u[2], copy_u[1]):
        copy.start()

    lane = lax.broadcasted_iota(jnp.int32, (RANK, ORDER), 1)
    copy_rows.wait()
    for u in range(UPD):
        column = jnp.broadcast_to(rows_v[pl.ds(u, 1), :], (128, RANK)).T[:, :1]
        s_ref[u] = jnp.where(lane == column, 1.0, 0.0).astype(BF16)

    copy_r.wait()
    r_hi, r_lo = split(r_v[...])
    for k in range(M_CHUNKS):
        copy_m[k].wait()
        m_hi, m_lo = split(m_v[pl.ds(k * size, size), :])
        p_ref[pl.ds(k * size, size), :] = mm_split(m_hi, m_lo, r_hi) + mm(m_hi, r_lo)
    copy_l.wait()
    for copy in copy_u:
        copy.wait()
    right = p_ref[...]
    left = l_v[...].T
    for early, late in ((0, 3), (1, 2)):
        right_hi, right_lo = split(right)
        picked_hi = mm(s_ref[early], right_hi).astype(BF16)
        picked_lo = mm(s_ref[early], right_lo).astype(BF16)
        right = right + (mm(u_v[early], picked_hi) + mm(u_v[early], picked_lo))
        left_hi, left_lo = split(left)
        x_hi, x_lo = split(mm_split(left_hi, left_lo, u_v[late]))
        left = left + mm_split(x_hi, x_lo, s_ref[late])
    left_hi, left_lo = split(left)
    right_hi, right_lo = split(right)
    out_ref[...] = mm_split(left_hi, left_lo, right_hi) + mm(left_hi, right_lo)


def walker(matrix, updates, rows, left, right):
    return pl.pallas_call(
        walker_kernel,
        out_shape=jax.ShapeDtypeStruct((KW, KW), F32),
        in_specs=[HBM] * 5,
        out_specs=VMEM,
        scratch_shapes=[
            pltpu.VMEM((ORDER, ORDER), F32),
            pltpu.VMEM((UPD, ORDER, RANK), BF16),
            pltpu.VMEM((UPD, RANK), jnp.int32),
            pltpu.VMEM((ORDER, KW), F32),
            pltpu.VMEM((ORDER, KW), F32),
            pltpu.VMEM((ORDER, KW), F32),
            pltpu.VMEM((UPD, RANK, ORDER), BF16),
            pltpu.SemaphoreType.DMA((3 + UPD + M_CHUNKS,)),
        ],
        compiler_params=pltpu.CompilerParams(vmem_limit_bytes=60 << 20),
        name="walker",
    )(matrix, updates, rows, left, right)


def route_kernel(n, targets_ref, x_ref, out_ref):
    for w in range(n):
        out_ref[targets_ref[0, w]] = x_ref[w]


def route(targets, chunks):
    return pl.pallas_call(
        functools.partial(route_kernel, chunks.shape[0]),
        out_shape=jax.ShapeDtypeStruct(chunks.shape, F32),
        in_specs=[SMEM, VMEM],
        out_specs=VMEM,
        compiler_params=pltpu.CompilerParams(vmem_limit_bytes=8 << 20),
        name="route",
    )(targets, chunks)


def labels_kernel(own_ref, ms_ref, tm_ref, tf_ref, pi_ref):
    lanes = lax.broadcasted_iota(jnp.int32, (NW, KW), 1)
    steps = lax.broadcasted_iota(jnp.int32, (NW, KW), 0)
    for j in range(own_ref.shape[0]):
        label = own_ref[j]
        moment = tm_ref[label]
        spot = (steps + tf_ref[label]) % NW
        for kappa in range(NK):
            goal = spot + ms_ref[kappa, moment] * NW
            pi_ref[pl.ds(j * KW + kappa * NW, NW), :] = jnp.where(lanes == goal, 1.0, 0.0).astype(BF16)


def labels(ownership, momentum_sum, moments, freqs):
    held = ownership.shape[0]
    return pl.pallas_call(
        labels_kernel,
        out_shape=jax.ShapeDtypeStruct((held * KW, KW), BF16),
        in_specs=[SMEM] * 4,
        out_specs=VMEM,
        cost_estimate=pl.CostEstimate(flops=4_000_000, bytes_accessed=1_000_000, transcendentals=0),
        compiler_params=pltpu.CompilerParams(vmem_limit_bytes=8 << 20),
        name="labels",
    )(ownership, momentum_sum, moments, freqs)


def products_kernel(scale, last, pi_ref, *refs):
    if last:
        *piece_refs, total_ref, out_hbm, out_v, sems = refs
    else:
        *piece_refs, total_ref, out_ref = refs
    held = total_ref.shape[0]
    pi = pi_ref[...]
    terms = [total_ref[j] for j in range(held)]
    for number, piece_ref in enumerate(piece_refs):
        a = piece_ref[...]
        a_hi, a_lo = split(a)
        v_hi = mm_nt(pi, a_hi).astype(BF16)
        v_lo = mm_nt(pi, a_lo).astype(BF16)
        a = a * scale
        for j in range(held):
            rows = slice(j * KW, (j + 1) * KW)
            terms[j] += a * (mm_nt(v_hi[rows], pi[rows]) + mm_nt(v_lo[rows], pi[rows]))
            if last and number == len(piece_refs) - 1:
                out_v[j] = terms[j]
                pltpu.make_async_copy(out_v.at[j], out_hbm.at[j], sems.at[j]).start()
    for j in range(held):
        if last:
            pltpu.make_async_copy(out_v.at[j], out_hbm.at[j], sems.at[j]).wait()
        else:
            out_ref[j] = terms[j]


def products(scale, pi, pieces, total, name, last=False):
    held = total.shape[0]
    count = len(pieces)
    return pl.pallas_call(
        functools.partial(products_kernel, scale, last),
        out_shape=jax.ShapeDtypeStruct(total.shape, F32),
        in_specs=[VMEM] * (2 + count),
        out_specs=HBM if last else VMEM,
        scratch_shapes=[pltpu.VMEM(total.shape, F32), pltpu.SemaphoreType.DMA((held,))] if last else [],
        cost_estimate=pl.CostEstimate(
            flops=count * held * 8 * KW**3, bytes_accessed=4 * KW * KW * (2 * held + count), transcendentals=0
        ),
        compiler_params=pltpu.CompilerParams(vmem_limit_bytes=16 << 20),
        name=name,
    )(pi, *pieces, total)


def cycle_products(scale, pi, own, prior):
    across = [(j, (j + 4) % 8) for j in range(8)]
    upward = [(j, j // 4 * 4 + (j % 4 + 1) % 4) for j in range(8)]
    downward = [(j, j // 4 * 4 + (j % 4 + 3) % 4) for j in range(8)]
    opposite = [(j, j // 4 * 4 + (j % 4 + 2) % 4) for j in range(8)]
    below = lax.ppermute(own, "blk", upward)
    above = lax.ppermute(own, "blk", downward)
    beside = lax.ppermute(own, "blk", across)
    far = lax.ppermute(own, "blk", opposite)
    total = products(scale, pi, [own], prior, "products_own")
    below, above, beside, far, total = lax.optimization_barrier((below, above, beside, far, total))
    beside_below = lax.ppermute(beside, "blk", upward)
    beside_above = lax.ppermute(beside, "blk", downward)
    beside_far = lax.ppermute(far, "blk", across)
    total = products(scale, pi, [below, above, beside, far], total, "products_near")
    total = products(scale, pi, [beside_below, beside_above], total, "products_beside")
    return products(scale, pi, [beside_far], total, "products_far", last=True)


def shards(
    walker_matrix, updates, update_rows, left_table, right_table, assignment, momentum_sum,
    transfer_momentum, transfer_frequency, ownership, g4_prior,
):
    n_grp = lax.axis_size("grp")
    pi = labels(ownership, momentum_sum, transfer_momentum, transfer_frequency)
    greens = walker(walker_matrix[0, 0], updates[0, 0], update_rows[0, 0], left_table, right_table)
    chunks = lax.all_to_all(greens.reshape(n_grp, KW // n_grp, KW), "grp", 0, 0, tiled=True)
    routed = route(assignment, chunks)
    measured = lax.all_to_all(routed, "grp", 0, 0, tiled=True).reshape(KW, KW)
    scale = 1.0 / lax.axis_size("blk")
    return cycle_products(scale, pi, measured, g4_prior[0])[None]


def solution(mesh):
    placed = (
        P("grp", "blk", None, None),
        P("grp", "blk", None, None, None),
        P("grp", "blk", None, None),
        P(),
        P(),
        P("blk", None),
        P(),
        P(),
        P(),
        P("blk"),
        P("grp", "blk", None, None),
    )
    return jax.shard_map(
        shards, mesh=mesh, in_specs=placed, out_specs=P("grp", "blk", None, None), check_vma=False
    )
```

```python
import functools

import jax
import jax.numpy as jnp
from jax import lax
from jax.experimental import pallas as pl
from jax.experimental.pallas import tpu as pltpu
from jax.sharding import PartitionSpec as P

UPD = 4
RANK = 256
ORDER = 1024
NW = 16
NK = 16
KW = 256
M_CHUNKS = 2
F32 = jnp.float32
BF16 = jnp.bfloat16

HBM = pl.BlockSpec(memory_space=pltpu.HBM)
VMEM = pl.BlockSpec(memory_space=pltpu.VMEM)
SMEM = pl.BlockSpec(memory_space=pltpu.SMEM)


def split(x):
    hi = x.astype(BF16)
    return hi, (x - hi.astype(F32)).astype(BF16)


def mm(a, b):
    return jnp.dot(a, b, preferred_element_type=F32)


def mm_nt(a, b):
    return lax.dot_general(a, b, (((1,), (1,)), ((), ())), preferred_element_type=F32)


def mm_split(hi, lo, b):
    count = hi.shape[0]
    both = mm(jnp.concatenate([hi, lo]), b)
    return both[:count] + both[count:]


def walker_kernel(m_hbm, u_hbm, rows_hbm, l_hbm, r_hbm, out_ref, m_v, u_v, rows_v, l_v, r_v, p_ref, s_ref, sems):
    size = ORDER // M_CHUNKS
    copy_rows = pltpu.make_async_copy(rows_hbm, rows_v, sems.at[0])
    copy_l = pltpu.make_async_copy(l_hbm, l_v, sems.at[1])
    copy_r = pltpu.make_async_copy(r_hbm, r_v, sems.at[2])
    copy_u = [pltpu.make_async_copy(u_hbm.at[u], u_v.at[u], sems.at[3 + u]) for u in range(UPD)]
    copy_m = [
        pltpu.make_async_copy(
            m_hbm.at[pl.ds(k * size, size), :], m_v.at[pl.ds(k * size, size), :], sems.at[3 + UPD + k]
        )
        for k in range(M_CHUNKS)
    ]
    for copy in (copy_rows, copy_r, *copy_m, copy_l, copy_u[3], copy_u[0], copy_u[2], copy_u[1]):
        copy.start()

    lane = lax.broadcasted_iota(jnp.int32, (RANK, ORDER), 1)
    copy_rows.wait()
    for u in range(UPD):
        column = jnp.broadcast_to(rows_v[pl.ds(u, 1), :], (128, RANK)).T[:, :1]
        s_ref[u] = jnp.where(lane == column, 1.0, 0.0).astype(BF16)

    copy_r.wait()
    r_hi, r_lo = split(r_v[...])
    for k in range(M_CHUNKS):
        copy_m[k].wait()
        m_hi, m_lo = split(m_v[pl.ds(k * size, size), :])
        p_ref[pl.ds(k * size, size), :] = mm_split(m_hi, m_lo, r_hi) + mm(m_hi, r_lo)
    copy_l.wait()
    for copy in copy_u:
        copy.wait()
    right = p_ref[...]
    left = l_v[...].T
    for early, late in ((0, 3), (1, 2)):
        right_hi, right_lo = split(right)
        picked_hi = mm(s_ref[early], right_hi).astype(BF16)
        picked_lo = mm(s_ref[early], right_lo).astype(BF16)
        right = right + (mm(u_v[early], picked_hi) + mm(u_v[early], picked_lo))
        left_hi, left_lo = split(left)
        x_hi, x_lo = split(mm_split(left_hi, left_lo, u_v[late]))
        left = left + mm_split(x_hi, x_lo, s_ref[late])
    left_hi, left_lo = split(left)
    right_hi, right_lo = split(right)
    out_ref[...] = mm_split(left_hi, left_lo, right_hi) + mm(left_hi, right_lo)


def walker(matrix, updates, rows, left, right):
    return pl.pallas_call(
        walker_kernel,
        out_shape=jax.ShapeDtypeStruct((KW, KW), F32),
        in_specs=[HBM] * 5,
        out_specs=VMEM,
        scratch_shapes=[
            pltpu.VMEM((ORDER, ORDER), F32),
            pltpu.VMEM((UPD, ORDER, RANK), BF16),
            pltpu.VMEM((UPD, RANK), jnp.int32),
            pltpu.VMEM((ORDER, KW), F32),
            pltpu.VMEM((ORDER, KW), F32),
            pltpu.VMEM((ORDER, KW), F32),
            pltpu.VMEM((UPD, RANK, ORDER), BF16),
            pltpu.SemaphoreType.DMA((3 + UPD + M_CHUNKS,)),
        ],
        compiler_params=pltpu.CompilerParams(vmem_limit_bytes=24 << 20),
        name="walker",
    )(*(pltpu.with_memory_space_constraint(x, pltpu.HBM) for x in (matrix, updates, rows, left, right)))


def route_kernel(n, targets_ref, x_ref, out_ref):
    for w in range(n):
        out_ref[targets_ref[0, w]] = x_ref[w]


def route(targets, chunks):
    return pl.pallas_call(
        functools.partial(route_kernel, chunks.shape[0]),
        out_shape=jax.ShapeDtypeStruct(chunks.shape, F32),
        in_specs=[SMEM, VMEM],
        out_specs=VMEM,
        compiler_params=pltpu.CompilerParams(vmem_limit_bytes=8 << 20),
        name="route",
    )(targets, chunks)


def labels_kernel(own_ref, ms_ref, tm_ref, tf_ref, pi_ref):
    lanes = lax.broadcasted_iota(jnp.int32, (NW, KW), 1)
    steps = lax.broadcasted_iota(jnp.int32, (NW, KW), 0)
    for j in range(own_ref.shape[0]):
        label = own_ref[j]
        moment = tm_ref[label]
        spot = (steps + tf_ref[label]) % NW
        for kappa in range(NK):
            goal = spot + ms_ref[kappa, moment] * NW
            pi_ref[pl.ds(j * KW + kappa * NW, NW), :] = jnp.where(lanes == goal, 1.0, 0.0).astype(BF16)


def labels(ownership, momentum_sum, moments, freqs):
    held = ownership.shape[0]
    return pl.pallas_call(
        labels_kernel,
        out_shape=jax.ShapeDtypeStruct((held * KW, KW), BF16),
        in_specs=[SMEM] * 4,
        out_specs=VMEM,
        cost_estimate=pl.CostEstimate(flops=4_000_000, bytes_accessed=1_000_000, transcendentals=0),
        compiler_params=pltpu.CompilerParams(vmem_limit_bytes=8 << 20),
        name="labels",
    )(ownership, momentum_sum, moments, freqs)


def products_kernel(scale, last, pi_ref, *refs):
    if last:
        *piece_refs, total_ref, out_hbm, out_v, sems = refs
    else:
        *piece_refs, total_ref, out_ref = refs
    held = total_ref.shape[0]
    pi = pi_ref[...]
    terms = [total_ref[j] for j in range(held)]
    for number, piece_ref in enumerate(piece_refs):
        a = piece_ref[...]
        a_hi, a_lo = split(a)
        v_hi = mm_nt(pi, a_hi).astype(BF16)
        v_lo = mm_nt(pi, a_lo).astype(BF16)
        a = a * scale
        for j in range(held):
            rows = slice(j * KW, (j + 1) * KW)
            terms[j] += a * (mm_nt(v_hi[rows], pi[rows]) + mm_nt(v_lo[rows], pi[rows]))
            if last and number == len(piece_refs) - 1:
                out_v[j] = terms[j]
                pltpu.make_async_copy(out_v.at[j], out_hbm.at[j], sems.at[j]).start()
    for j in range(held):
        if last:
            pltpu.make_async_copy(out_v.at[j], out_hbm.at[j], sems.at[j]).wait()
        else:
            out_ref[j] = terms[j]


def products(scale, pi, pieces, total, name, last=False):
    held = total.shape[0]
    count = len(pieces)
    return pl.pallas_call(
        functools.partial(products_kernel, scale, last),
        out_shape=jax.ShapeDtypeStruct(total.shape, F32),
        in_specs=[VMEM] * (2 + count),
        out_specs=HBM if last else VMEM,
        scratch_shapes=[pltpu.VMEM(total.shape, F32), pltpu.SemaphoreType.DMA((held,))] if last else [],
        cost_estimate=pl.CostEstimate(
            flops=count * held * 8 * KW**3, bytes_accessed=4 * KW * KW * (2 * held + count), transcendentals=0
        ),
        compiler_params=pltpu.CompilerParams(vmem_limit_bytes=16 << 20),
        name=name,
    )(pi, *pieces, total)


def cycle_products(scale, pi, own, prior):
    across = [(j, (j + 4) % 8) for j in range(8)]
    upward = [(j, j // 4 * 4 + (j % 4 + 1) % 4) for j in range(8)]
    downward = [(j, j // 4 * 4 + (j % 4 + 3) % 4) for j in range(8)]
    opposite = [(j, j // 4 * 4 + (j % 4 + 2) % 4) for j in range(8)]
    below = lax.ppermute(own, "blk", upward)
    above = lax.ppermute(own, "blk", downward)
    beside = lax.ppermute(own, "blk", across)
    far = lax.ppermute(own, "blk", opposite)
    total = products(scale, pi, [own], prior, "products_own")
    beside, total = lax.optimization_barrier((beside, total))
    beside_below = lax.ppermute(beside, "blk", upward)
    beside_above = lax.ppermute(beside, "blk", downward)
    far, total = lax.optimization_barrier((far, total))
    beside_far = lax.ppermute(far, "blk", across)
    total = products(scale, pi, [beside, far, below, above], total, "products_near")
    total = products(scale, pi, [beside_below, beside_above], total, "products_beside")
    return products(scale, pi, [beside_far], total, "products_far", last=True)


def shards(
    walker_matrix, updates, update_rows, left_table, right_table, assignment, momentum_sum,
    transfer_momentum, transfer_frequency, ownership, g4_prior,
):
    n_grp = lax.axis_size("grp")
    pi = labels(ownership, momentum_sum, transfer_momentum, transfer_frequency)
    greens = walker(walker_matrix[0, 0], updates[0, 0], update_rows[0, 0], left_table, right_table)
    chunks = lax.all_to_all(greens.reshape(n_grp, KW // n_grp, KW), "grp", 0, 0, tiled=True)
    routed = route(assignment, chunks)
    measured = lax.all_to_all(routed, "grp", 0, 0, tiled=True).reshape(KW, KW)
    scale = 1.0 / lax.axis_size("blk")
    return cycle_products(scale, pi, measured, g4_prior[0])[None]


def solution(mesh):
    placed = (
        P("grp", "blk", None, None),
        P("grp", "blk", None, None, None),
        P("grp", "blk", None, None),
        P(),
        P(),
        P("blk", None),
        P(),
        P(),
        P(),
        P("blk"),
        P("grp", "blk", None, None),
    )
    return jax.shard_map(
        shards, mesh=mesh, in_specs=placed, out_specs=P("grp", "blk", None, None), check_vma=False
    )
```

```python
import functools

import jax
import jax.numpy as jnp
from jax import lax
from jax.experimental import pallas as pl
from jax.experimental.pallas import tpu as pltpu
from jax.sharding import PartitionSpec as P

UPD = 4
RANK = 256
ORDER = 1024
NW = 16
NK = 16
KW = 256
M_FIRST = 768
F32 = jnp.float32
BF16 = jnp.bfloat16

HBM = pl.BlockSpec(memory_space=pltpu.HBM)
VMEM = pl.BlockSpec(memory_space=pltpu.VMEM)
SMEM = pl.BlockSpec(memory_space=pltpu.SMEM)


def split(x):
    hi = x.astype(BF16)
    return hi, (x - hi.astype(F32)).astype(BF16)


def mm(a, b):
    return jnp.dot(a, b, preferred_element_type=F32)


def mm_nt(a, b):
    return lax.dot_general(a, b, (((1,), (1,)), ((), ())), preferred_element_type=F32)


def mm_split(hi, lo, b, product=mm):
    count = hi.shape[0]
    both = product(jnp.concatenate([hi, lo]), b)
    return both[:count] + both[count:]


def walker_kernel(m_hbm, u_hbm, rows_hbm, l_hbm, r_hbm, out_ref, m_v, u_v, rows_v, l_v, r_v, p_ref, s_ref, sems):
    copy_rows = pltpu.make_async_copy(rows_hbm, rows_v, sems.at[0])
    copy_l = pltpu.make_async_copy(l_hbm, l_v, sems.at[1])
    copy_r = pltpu.make_async_copy(r_hbm, r_v, sems.at[2])
    copy_u = [pltpu.make_async_copy(u_hbm.at[u], u_v.at[u], sems.at[3 + u]) for u in range(UPD)]
    spans = [pl.ds(0, M_FIRST), pl.ds(M_FIRST, ORDER - M_FIRST)]
    copy_m = [
        pltpu.make_async_copy(m_hbm.at[span, :], m_v.at[span, :], sems.at[3 + UPD + k])
        for k, span in enumerate(spans)
    ]
    for copy in (copy_rows, copy_r, *copy_m, copy_l, copy_u[3], copy_u[2], copy_u[0], copy_u[1]):
        copy.start()

    lane = lax.broadcasted_iota(jnp.int32, (RANK, ORDER), 1)
    copy_rows.wait()
    for u in range(UPD):
        column = jnp.broadcast_to(rows_v[pl.ds(u, 1), :], (128, RANK)).T[:, :1]
        s_ref[u] = jnp.where(lane == column, 1.0, 0.0).astype(BF16)

    copy_r.wait()
    r_hi, r_lo = split(r_v[...].T)

    def multiply(span):
        m_hi, m_lo = split(m_v[span, :])
        p_ref[:, span] = mm_split(r_hi, r_lo, m_hi, mm_nt) + mm_nt(r_hi, m_lo)

    copy_m[0].wait()
    multiply(spans[0])
    for copy in (copy_m[1], copy_l, *copy_u):
        copy.wait()
    left = l_v[...].T
    multiply(spans[1])
    right = p_ref[...]
    for early, late in ((0, 3), (1, 2)):
        right_hi, right_lo = split(right)
        x_hi, x_lo = split(mm_split(right_hi, right_lo, s_ref[early], mm_nt))
        right = right + mm_split(x_hi, x_lo, u_v[early], mm_nt)
        left_hi, left_lo = split(left)
        x_hi, x_lo = split(mm_split(left_hi, left_lo, u_v[late]))
        left = left + mm_split(x_hi, x_lo, s_ref[late])
    left_hi, left_lo = split(left)
    right_hi, right_lo = split(right)
    out_ref[...] = mm_split(left_hi, left_lo, right_hi, mm_nt) + mm_nt(left_hi, right_lo)


def walker(matrix, updates, rows, left, right):
    return pl.pallas_call(
        walker_kernel,
        out_shape=jax.ShapeDtypeStruct((KW, KW), F32),
        in_specs=[HBM] * 5,
        out_specs=VMEM,
        scratch_shapes=[
            pltpu.VMEM((ORDER, ORDER), F32),
            pltpu.VMEM((UPD, ORDER, RANK), BF16),
            pltpu.VMEM((UPD, RANK), jnp.int32),
            pltpu.VMEM((ORDER, KW), F32),
            pltpu.VMEM((ORDER, KW), F32),
            pltpu.VMEM((KW, ORDER), F32),
            pltpu.VMEM((UPD, RANK, ORDER), BF16),
            pltpu.SemaphoreType.DMA((5 + UPD,)),
        ],
        compiler_params=pltpu.CompilerParams(vmem_limit_bytes=24 << 20),
        name="walker",
    )(*(pltpu.with_memory_space_constraint(x, pltpu.HBM) for x in (matrix, updates, rows, left, right)))


def route_kernel(n, targets_ref, x_ref, out_ref):
    for w in range(n):
        out_ref[targets_ref[0, w]] = x_ref[w]


def route(targets, chunks):
    return pl.pallas_call(
        functools.partial(route_kernel, chunks.shape[0]),
        out_shape=jax.ShapeDtypeStruct(chunks.shape, F32),
        in_specs=[SMEM, VMEM],
        out_specs=VMEM,
        compiler_params=pltpu.CompilerParams(vmem_limit_bytes=8 << 20),
        name="route",
    )(targets, chunks)


def labels_kernel(own_ref, ms_ref, tm_ref, tf_ref, pi_ref):
    lanes = lax.broadcasted_iota(jnp.int32, (NW, KW), 1)
    steps = lax.broadcasted_iota(jnp.int32, (NW, KW), 0)
    for j in range(own_ref.shape[0]):
        label = own_ref[j]
        moment = tm_ref[label]
        spot = (steps + tf_ref[label]) % NW
        for kappa in range(NK):
            goal = spot + ms_ref[kappa, moment] * NW
            pi_ref[pl.ds(j * KW + kappa * NW, NW), :] = jnp.where(lanes == goal, 1.0, 0.0).astype(BF16)


def labels(ownership, momentum_sum, moments, freqs):
    held = ownership.shape[0]
    return pl.pallas_call(
        labels_kernel,
        out_shape=jax.ShapeDtypeStruct((held * KW, KW), BF16),
        in_specs=[SMEM] * 4,
        out_specs=VMEM,
        cost_estimate=pl.CostEstimate(flops=4_000_000, bytes_accessed=1_000_000, transcendentals=0),
        compiler_params=pltpu.CompilerParams(vmem_limit_bytes=8 << 20),
        name="labels",
    )(ownership, momentum_sum, moments, freqs)


def products_kernel(scale, last, pi_ref, *refs):
    if last:
        *piece_refs, total_ref, out_hbm, out_v, sems = refs
    else:
        *piece_refs, total_ref, out_ref = refs
    held = total_ref.shape[0]
    pi = pi_ref[...]
    terms = [total_ref[j] for j in range(held)]
    for number, piece_ref in enumerate(piece_refs):
        a = piece_ref[...]
        a_hi, a_lo = split(a)
        v_hi = mm_nt(pi, a_hi).astype(BF16)
        v_lo = mm_nt(pi, a_lo).astype(BF16)
        a = a * scale
        for j in range(held):
            rows = slice(j * KW, (j + 1) * KW)
            terms[j] += a * (mm_nt(v_hi[rows], pi[rows]) + mm_nt(v_lo[rows], pi[rows]))
            if last and number == len(piece_refs) - 1:
                out_v[j] = terms[j]
                pltpu.make_async_copy(out_v.at[j], out_hbm.at[j], sems.at[j]).start()
    for j in range(held):
        if last:
            pltpu.make_async_copy(out_v.at[j], out_hbm.at[j], sems.at[j]).wait()
        else:
            out_ref[j] = terms[j]


def products(scale, pi, pieces, total, name, last=False):
    held = total.shape[0]
    count = len(pieces)
    return pl.pallas_call(
        functools.partial(products_kernel, scale, last),
        out_shape=jax.ShapeDtypeStruct(total.shape, F32),
        in_specs=[VMEM] * (2 + count),
        out_specs=HBM if last else VMEM,
        scratch_shapes=[pltpu.VMEM(total.shape, F32), pltpu.SemaphoreType.DMA((held,))] if last else [],
        cost_estimate=pl.CostEstimate(
            flops=count * held * 8 * KW**3, bytes_accessed=4 * KW * KW * (2 * held + count), transcendentals=0
        ),
        compiler_params=pltpu.CompilerParams(vmem_limit_bytes=16 << 20),
        name=name,
    )(pi, *pieces, total)


def cycle_products(scale, pi, own, prior):
    across = [(j, (j + 4) % 8) for j in range(8)]
    upward = [(j, j // 4 * 4 + (j % 4 + 1) % 4) for j in range(8)]
    downward = [(j, j // 4 * 4 + (j % 4 + 3) % 4) for j in range(8)]
    opposite = [(j, j // 4 * 4 + (j % 4 + 2) % 4) for j in range(8)]
    far = lax.ppermute(own, "blk", opposite)
    beside = lax.ppermute(own, "blk", across)
    below = lax.ppermute(own, "blk", upward)
    above = lax.ppermute(own, "blk", downward)
    total = products(scale, pi, [own], prior, "products_own")
    far, total = lax.optimization_barrier((far, total))
    beside_far = lax.ppermute(far, "blk", across)
    beside, total = lax.optimization_barrier((beside, total))
    beside_below = lax.ppermute(beside, "blk", upward)
    beside_above = lax.ppermute(beside, "blk", downward)
    total = products(scale, pi, [beside, far, below, above], total, "products_near")
    total = products(scale, pi, [beside_far], total, "products_far")
    return products(scale, pi, [beside_below, beside_above], total, "products_last", last=True)


def shards(
    walker_matrix, updates, update_rows, left_table, right_table, assignment, momentum_sum,
    transfer_momentum, transfer_frequency, ownership, g4_prior,
):
    n_grp = lax.axis_size("grp")
    pi = labels(ownership, momentum_sum, transfer_momentum, transfer_frequency)
    greens = walker(walker_matrix[0, 0], updates[0, 0], update_rows[0, 0], left_table, right_table)
    chunks = lax.all_to_all(greens.reshape(n_grp, KW // n_grp, KW), "grp", 0, 0, tiled=True)
    routed = route(assignment, chunks)
    measured = lax.all_to_all(routed, "grp", 0, 0, tiled=True).reshape(KW, KW)
    scale = 1.0 / lax.axis_size("blk")
    return cycle_products(scale, pi, measured, g4_prior[0])[None]


def solution(mesh):
    placed = (
        P("grp", "blk", None, None),
        P("grp", "blk", None, None, None),
        P("grp", "blk", None, None),
        P(),
        P(),
        P("blk", None),
        P(),
        P(),
        P(),
        P("blk"),
        P("grp", "blk", None, None),
    )
    return jax.shard_map(
        shards, mesh=mesh, in_specs=placed, out_specs=P("grp", "blk", None, None), check_vma=False
    )
```

```python
import functools

import jax
import jax.numpy as jnp
from jax import lax
from jax.experimental import pallas as pl
from jax.experimental.pallas import tpu as pltpu
from jax.sharding import PartitionSpec as P

UPD = 4
RANK = 256
ORDER = 1024
NW = 16
NK = 16
KW = 256
M_FIRST = 768
F32 = jnp.float32
BF16 = jnp.bfloat16

HBM = pl.BlockSpec(memory_space=pltpu.HBM)
VMEM = pl.BlockSpec(memory_space=pltpu.VMEM)
SMEM = pl.BlockSpec(memory_space=pltpu.SMEM)


def split(x):
    hi = x.astype(BF16)
    return hi, (x - hi.astype(F32)).astype(BF16)


def mm(a, b):
    return jnp.dot(a, b, preferred_element_type=F32)


def mm_nt(a, b):
    return lax.dot_general(a, b, (((1,), (1,)), ((), ())), preferred_element_type=F32)


def mm_split(hi, lo, b, product=mm):
    count = hi.shape[0]
    both = product(jnp.concatenate([hi, lo]), b)
    return both[:count] + both[count:]


def walker_kernel(m_hbm, u_hbm, rows_hbm, l_hbm, r_hbm, out_ref, m_v, u_v, rows_v, l_v, r_v, p_ref, s_ref, sems):
    copy_rows = pltpu.make_async_copy(rows_hbm, rows_v, sems.at[0])
    copy_l = pltpu.make_async_copy(l_hbm, l_v, sems.at[1])
    copy_r = pltpu.make_async_copy(r_hbm, r_v, sems.at[2])
    copy_u = [pltpu.make_async_copy(u_hbm.at[u], u_v.at[u], sems.at[3 + u]) for u in range(UPD)]
    spans = [pl.ds(0, M_FIRST), pl.ds(M_FIRST, ORDER - M_FIRST)]
    copy_m = [
        pltpu.make_async_copy(m_hbm.at[span, :], m_v.at[span, :], sems.at[3 + UPD + k])
        for k, span in enumerate(spans)
    ]
    for copy in (copy_rows, copy_r, *copy_m, copy_l, copy_u[3], copy_u[2], copy_u[0], copy_u[1]):
        copy.start()

    lane = lax.broadcasted_iota(jnp.int32, (RANK, ORDER), 1)
    copy_rows.wait()
    for u in range(UPD):
        column = jnp.broadcast_to(rows_v[pl.ds(u, 1), :], (128, RANK)).T[:, :1]
        s_ref[u] = jnp.where(lane == column, 1.0, 0.0).astype(BF16)

    copy_r.wait()
    r_hi, r_lo = split(r_v[...].T)

    def multiply(span):
        m_hi, m_lo = split(m_v[span, :])
        p_ref[:, span] = mm_split(r_hi, r_lo, m_hi, mm_nt) + mm_nt(r_hi, m_lo)

    copy_m[0].wait()
    multiply(spans[0])
    for copy in (copy_m[1], copy_l, *copy_u):
        copy.wait()
    left = l_v[...].T
    multiply(spans[1])
    right = p_ref[...]
    for early, late in ((0, 3), (1, 2)):
        right_hi, right_lo = split(right)
        x_hi, x_lo = split(mm_split(right_hi, right_lo, s_ref[early], mm_nt))
        right = right + mm_split(x_hi, x_lo, u_v[early], mm_nt)
        left_hi, left_lo = split(left)
        x_hi, x_lo = split(mm_split(left_hi, left_lo, u_v[late]))
        left = left + mm_split(x_hi, x_lo, s_ref[late])
    left_hi, left_lo = split(left)
    right_hi, right_lo = split(right)
    out_ref[...] = mm_split(left_hi, left_lo, right_hi, mm_nt) + mm_nt(left_hi, right_lo)


def walker(matrix, updates, rows, left, right):
    return pl.pallas_call(
        walker_kernel,
        out_shape=jax.ShapeDtypeStruct((KW, KW), F32),
        in_specs=[HBM] * 5,
        out_specs=VMEM,
        scratch_shapes=[
            pltpu.VMEM((ORDER, ORDER), F32),
            pltpu.VMEM((UPD, ORDER, RANK), BF16),
            pltpu.VMEM((UPD, RANK), jnp.int32),
            pltpu.VMEM((ORDER, KW), F32),
            pltpu.VMEM((ORDER, KW), F32),
            pltpu.VMEM((KW, ORDER), F32),
            pltpu.VMEM((UPD, RANK, ORDER), BF16),
            pltpu.SemaphoreType.DMA((5 + UPD,)),
        ],
        compiler_params=pltpu.CompilerParams(vmem_limit_bytes=24 << 20),
        name="walker",
    )(*(pltpu.with_memory_space_constraint(x, pltpu.HBM) for x in (matrix, updates, rows, left, right)))


def route_kernel(core_ref, targets_ref, own_ref, other_ref, out_ref):
    core = core_ref[0]
    for pair in range(own_ref.shape[0]):
        for part, source_ref in ((core, own_ref), (1 - core, other_ref)):
            target = targets_ref[0, 2 * pair + part]

            @pl.when((target & 1) == core)
            def _():
                out_ref[target >> 1] = source_ref[pair]


def route(core, targets, own, other):
    return pl.pallas_call(
        route_kernel,
        out_shape=jax.ShapeDtypeStruct(own.shape, F32),
        in_specs=[SMEM, SMEM, VMEM, VMEM],
        out_specs=VMEM,
        compiler_params=pltpu.CompilerParams(vmem_limit_bytes=8 << 20),
        name="route",
    )(core, targets, own, other)


def permute_walkers(greens, targets):
    n_grp = lax.axis_size("grp")
    pairs = n_grp // 2
    core = lax.axis_index("grp") & 1
    alike = [[2 * pair + part for pair in range(pairs)] for part in range(2)]
    chunks = greens.reshape(pairs, KW // pairs, KW)
    own = lax.all_to_all(chunks, "grp", 0, 0, axis_index_groups=alike, tiled=True)
    other = lax.ppermute(own, "grp", [(w, w ^ 1) for w in range(n_grp)])
    routed = route(core.reshape(1), targets, own, other)
    return lax.all_to_all(routed, "grp", 0, 0, axis_index_groups=alike, tiled=True).reshape(KW, KW)


def labels_kernel(own_ref, ms_ref, tm_ref, tf_ref, pi_ref):
    lanes = lax.broadcasted_iota(jnp.int32, (NW, KW), 1)
    steps = lax.broadcasted_iota(jnp.int32, (NW, KW), 0)
    for j in range(own_ref.shape[0]):
        label = own_ref[j]
        moment = tm_ref[label]
        spot = (steps + tf_ref[label]) % NW
        for kappa in range(NK):
            goal = spot + ms_ref[kappa, moment] * NW
            pi_ref[pl.ds(j * KW + kappa * NW, NW), :] = jnp.where(lanes == goal, 1.0, 0.0).astype(BF16)


def labels(ownership, momentum_sum, moments, freqs):
    held = ownership.shape[0]
    return pl.pallas_call(
        labels_kernel,
        out_shape=jax.ShapeDtypeStruct((held * KW, KW), BF16),
        in_specs=[SMEM] * 4,
        out_specs=VMEM,
        cost_estimate=pl.CostEstimate(flops=4_000_000, bytes_accessed=1_000_000, transcendentals=0),
        compiler_params=pltpu.CompilerParams(vmem_limit_bytes=8 << 20),
        name="labels",
    )(ownership, momentum_sum, moments, freqs)


def products_kernel(scale, last, pi_ref, *refs):
    if last:
        *piece_refs, total_ref, out_hbm, out_v, sems = refs
    else:
        *piece_refs, total_ref, out_ref = refs
    held = total_ref.shape[0]
    pi = pi_ref[...]
    blocks = []
    for piece_ref in piece_refs:
        a_hi, a_lo = split(piece_ref[...])
        blocks.append((mm_nt(pi, a_hi).astype(BF16), mm_nt(pi, a_lo).astype(BF16)))
    for j in range(held):
        rows = slice(j * KW, (j + 1) * KW)
        term = total_ref[j]
        for piece_ref, (v_hi, v_lo) in zip(piece_refs, blocks):
            term += piece_ref[...] * scale * (mm_nt(v_hi[rows], pi[rows]) + mm_nt(v_lo[rows], pi[rows]))
        if last:
            out_v[j] = term
            pltpu.make_async_copy(out_v.at[j], out_hbm.at[j], sems.at[j]).start()
        else:
            out_ref[j] = term
    if last:
        for j in range(held):
            pltpu.make_async_copy(out_v.at[j], out_hbm.at[j], sems.at[j]).wait()


def products(scale, pi, pieces, total, name, last=False):
    held = total.shape[0]
    count = len(pieces)
    return pl.pallas_call(
        functools.partial(products_kernel, scale, last),
        out_shape=jax.ShapeDtypeStruct(total.shape, F32),
        in_specs=[VMEM] * (2 + count),
        out_specs=HBM if last else VMEM,
        scratch_shapes=[pltpu.VMEM(total.shape, F32), pltpu.SemaphoreType.DMA((held,))] if last else [],
        cost_estimate=pl.CostEstimate(
            flops=count * held * 8 * KW**3, bytes_accessed=4 * KW * KW * (2 * held + count), transcendentals=0
        ),
        compiler_params=pltpu.CompilerParams(vmem_limit_bytes=16 << 20),
        name=name,
    )(pi, *pieces, total)


def cycle_products(scale, pi, own, prior):
    across = [(j, (j + 4) % 8) for j in range(8)]
    upward = [(j, j // 4 * 4 + (j % 4 + 1) % 4) for j in range(8)]
    downward = [(j, j // 4 * 4 + (j % 4 + 3) % 4) for j in range(8)]
    opposite = [(j, j // 4 * 4 + (j % 4 + 2) % 4) for j in range(8)]
    far = lax.ppermute(own, "blk", opposite)
    beside = lax.ppermute(own, "blk", across)
    below = lax.ppermute(own, "blk", upward)
    above = lax.ppermute(own, "blk", downward)
    total = products(scale, pi, [own], prior, "products_own")
    far, total = lax.optimization_barrier((far, total))
    beside_far = lax.ppermute(far, "blk", across)
    beside, total = lax.optimization_barrier((beside, total))
    beside_below = lax.ppermute(beside, "blk", upward)
    beside_above = lax.ppermute(beside, "blk", downward)
    total = products(scale, pi, [beside, far, below, above], total, "products_near")
    total = products(scale, pi, [beside_far], total, "products_far")
    return products(scale, pi, [beside_below, beside_above], total, "products_last", last=True)


def shards(
    walker_matrix, updates, update_rows, left_table, right_table, assignment, momentum_sum,
    transfer_momentum, transfer_frequency, ownership, g4_prior,
):
    pi = labels(ownership, momentum_sum, transfer_momentum, transfer_frequency)
    greens = walker(walker_matrix[0, 0], updates[0, 0], update_rows[0, 0], left_table, right_table)
    measured = permute_walkers(greens, assignment)
    scale = 1.0 / lax.axis_size("blk")
    return cycle_products(scale, pi, measured, g4_prior[0])[None]


def solution(mesh):
    placed = (
        P("grp", "blk", None, None),
        P("grp", "blk", None, None, None),
        P("grp", "blk", None, None),
        P(),
        P(),
        P("blk", None),
        P(),
        P(),
        P(),
        P("blk"),
        P("grp", "blk", None, None),
    )
    return jax.shard_map(
        shards, mesh=mesh, in_specs=placed, out_specs=P("grp", "blk", None, None), check_vma=False
    )
```

```python
import functools

import jax
import jax.numpy as jnp
from jax import lax
from jax.experimental import pallas as pl
from jax.experimental.pallas import tpu as pltpu
from jax.sharding import PartitionSpec as P

UPD = 4
RANK = 256
ORDER = 1024
NW = 16
NK = 16
KW = 256
M_FIRST = 768
F32 = jnp.float32
BF16 = jnp.bfloat16

HBM = pl.BlockSpec(memory_space=pltpu.HBM)
VMEM = pl.BlockSpec(memory_space=pltpu.VMEM)
SMEM = pl.BlockSpec(memory_space=pltpu.SMEM)


def split(x):
    hi = x.astype(BF16)
    return hi, (x - hi.astype(F32)).astype(BF16)


def mm(a, b):
    return jnp.dot(a, b, preferred_element_type=F32)


def mm_nt(a, b):
    return lax.dot_general(a, b, (((1,), (1,)), ((), ())), preferred_element_type=F32)


def mm_split(hi, lo, b, product=mm):
    count = hi.shape[0]
    both = product(jnp.concatenate([hi, lo]), b)
    return both[:count] + both[count:]


def walker_kernel(m_hbm, u_hbm, rows_hbm, l_hbm, r_hbm, out_ref, m_v, u_v, rows_v, l_v, r_v, p_ref, s_ref, sems):
    copy_rows = pltpu.make_async_copy(rows_hbm, rows_v, sems.at[0])
    copy_l = pltpu.make_async_copy(l_hbm, l_v, sems.at[1])
    copy_r = pltpu.make_async_copy(r_hbm, r_v, sems.at[2])
    copy_u = [pltpu.make_async_copy(u_hbm.at[u], u_v.at[u], sems.at[3 + u]) for u in range(UPD)]
    spans = [pl.ds(0, M_FIRST), pl.ds(M_FIRST, ORDER - M_FIRST)]
    copy_m = [
        pltpu.make_async_copy(m_hbm.at[span, :], m_v.at[span, :], sems.at[3 + UPD + k])
        for k, span in enumerate(spans)
    ]
    for copy in (copy_rows, copy_r, *copy_m, copy_l, copy_u[3], copy_u[2], copy_u[0], copy_u[1]):
        copy.start()

    lane = lax.broadcasted_iota(jnp.int32, (RANK, ORDER), 1)
    copy_rows.wait()
    for u in range(UPD):
        column = jnp.broadcast_to(rows_v[pl.ds(u, 1), :], (128, RANK)).T[:, :1]
        s_ref[u] = jnp.where(lane == column, 1.0, 0.0).astype(BF16)

    copy_r.wait()
    r_hi, r_lo = split(r_v[...].T)

    def multiply(span):
        m_hi, m_lo = split(m_v[span, :])
        p_ref[:, span] = mm_split(r_hi, r_lo, m_hi, mm_nt) + mm_nt(r_hi, m_lo)

    copy_m[0].wait()
    multiply(spans[0])
    for copy in (copy_m[1], copy_l, *copy_u):
        copy.wait()
    left = l_v[...].T
    multiply(spans[1])
    right = p_ref[...]
    for early, late in ((0, 3), (1, 2)):
        right_hi, right_lo = split(right)
        x_hi, x_lo = split(mm_split(right_hi, right_lo, s_ref[early], mm_nt))
        right = right + mm_split(x_hi, x_lo, u_v[early], mm_nt)
        left_hi, left_lo = split(left)
        x_hi, x_lo = split(mm_split(left_hi, left_lo, u_v[late]))
        left = left + mm_split(x_hi, x_lo, s_ref[late])
    left_hi, left_lo = split(left)
    right_hi, right_lo = split(right)
    out_ref[...] = mm_split(left_hi, left_lo, right_hi, mm_nt) + mm_nt(left_hi, right_lo)


def walker(matrix, updates, rows, left, right):
    return pl.pallas_call(
        walker_kernel,
        out_shape=jax.ShapeDtypeStruct((KW, KW), F32),
        in_specs=[HBM] * 5,
        out_specs=VMEM,
        scratch_shapes=[
            pltpu.VMEM((ORDER, ORDER), F32),
            pltpu.VMEM((UPD, ORDER, RANK), BF16),
            pltpu.VMEM((UPD, RANK), jnp.int32),
            pltpu.VMEM((ORDER, KW), F32),
            pltpu.VMEM((ORDER, KW), F32),
            pltpu.VMEM((KW, ORDER), F32),
            pltpu.VMEM((UPD, RANK, ORDER), BF16),
            pltpu.SemaphoreType.DMA((5 + UPD,)),
        ],
        compiler_params=pltpu.CompilerParams(vmem_limit_bytes=24 << 20),
        name="walker",
    )(*(pltpu.with_memory_space_constraint(x, pltpu.HBM) for x in (matrix, updates, rows, left, right)))


def route_kernel(core_ref, targets_ref, own_ref, other_ref, out_ref):
    core = core_ref[0]
    for pair in range(own_ref.shape[0]):
        for part, source_ref in ((core, own_ref), (1 - core, other_ref)):
            target = targets_ref[0, 2 * pair + part]

            @pl.when((target & 1) == core)
            def _():
                out_ref[target >> 1] = source_ref[pair]


def route(core, targets, own, other):
    return pl.pallas_call(
        route_kernel,
        out_shape=jax.ShapeDtypeStruct(own.shape, F32),
        in_specs=[SMEM, SMEM, VMEM, VMEM],
        out_specs=VMEM,
        compiler_params=pltpu.CompilerParams(vmem_limit_bytes=8 << 20),
        name="route",
    )(core, targets, own, other)


def permute_walkers(greens, targets):
    n_grp = lax.axis_size("grp")
    pairs = n_grp // 2
    core = lax.axis_index("grp") & 1
    alike = [[2 * pair + part for pair in range(pairs)] for part in range(2)]
    chunks = greens.reshape(pairs, KW // pairs, KW)
    own = lax.all_to_all(chunks, "grp", 0, 0, axis_index_groups=alike, tiled=True)
    other = lax.ppermute(own, "grp", [(w, w ^ 1) for w in range(n_grp)])
    routed = route(core.reshape(1), targets, own, other)
    return lax.all_to_all(routed, "grp", 0, 0, axis_index_groups=alike, tiled=True).reshape(KW, KW)


def labels_kernel(own_ref, ms_ref, tm_ref, tf_ref, pi_ref):
    lanes = lax.broadcasted_iota(jnp.int32, (NW, KW), 1)
    steps = lax.broadcasted_iota(jnp.int32, (NW, KW), 0)
    for j in range(own_ref.shape[0]):
        label = own_ref[j]
        moment = tm_ref[label]
        spot = (steps + tf_ref[label]) % NW
        for kappa in range(NK):
            goal = spot + ms_ref[kappa, moment] * NW
            pi_ref[pl.ds(j * KW + kappa * NW, NW), :] = jnp.where(lanes == goal, 1.0, 0.0).astype(BF16)


def labels(ownership, momentum_sum, moments, freqs):
    held = ownership.shape[0]
    return pl.pallas_call(
        labels_kernel,
        out_shape=jax.ShapeDtypeStruct((held * KW, KW), BF16),
        in_specs=[SMEM] * 4,
        out_specs=VMEM,
        cost_estimate=pl.CostEstimate(flops=4_000_000, bytes_accessed=1_000_000, transcendentals=0),
        compiler_params=pltpu.CompilerParams(vmem_limit_bytes=8 << 20),
        name="labels",
    )(ownership, momentum_sum, moments, freqs)


def products_kernel(scale, last, pi_ref, *refs):
    if last:
        *piece_refs, total_ref, out_hbm, out_v, sems = refs
    else:
        *piece_refs, total_ref, out_ref = refs
    held = total_ref.shape[0]
    pi = pi_ref[...]
    blocks = []
    for piece_ref in piece_refs:
        a_hi, a_lo = split(piece_ref[...])
        blocks.append((mm_nt(pi, a_hi).astype(BF16), mm_nt(pi, a_lo).astype(BF16)))
    for j in range(held):
        rows = slice(j * KW, (j + 1) * KW)
        term = total_ref[j]
        for piece_ref, (v_hi, v_lo) in zip(piece_refs, blocks):
            term += piece_ref[...] * scale * (mm_nt(v_hi[rows], pi[rows]) + mm_nt(v_lo[rows], pi[rows]))
        if last:
            out_v[j] = term
            pltpu.make_async_copy(out_v.at[j], out_hbm.at[j], sems.at[j]).start()
        else:
            out_ref[j] = term
    if last:
        for j in range(held):
            pltpu.make_async_copy(out_v.at[j], out_hbm.at[j], sems.at[j]).wait()


def products(scale, pi, pieces, total, name, last=False):
    held = total.shape[0]
    count = len(pieces)
    return pl.pallas_call(
        functools.partial(products_kernel, scale, last),
        out_shape=jax.ShapeDtypeStruct(total.shape, F32),
        in_specs=[VMEM] * (2 + count),
        out_specs=HBM if last else VMEM,
        scratch_shapes=[pltpu.VMEM(total.shape, F32), pltpu.SemaphoreType.DMA((held,))] if last else [],
        cost_estimate=pl.CostEstimate(
            flops=count * held * 8 * KW**3, bytes_accessed=4 * KW * KW * (2 * held + count), transcendentals=0
        ),
        compiler_params=pltpu.CompilerParams(vmem_limit_bytes=16 << 20),
        name=name,
    )(pi, *pieces, total)


def cycle_products(scale, pi, own, prior):
    across = [(j, (j + 4) % 8) for j in range(8)]
    upward = [(j, j // 4 * 4 + (j % 4 + 1) % 4) for j in range(8)]
    downward = [(j, j // 4 * 4 + (j % 4 + 3) % 4) for j in range(8)]
    opposite = [(j, j // 4 * 4 + (j % 4 + 2) % 4) for j in range(8)]
    far = lax.ppermute(own, "blk", opposite)
    beside = lax.ppermute(own, "blk", across)
    below = lax.ppermute(own, "blk", upward)
    above = lax.ppermute(own, "blk", downward)
    total = products(scale, pi, [own], prior, "products_own")
    far, total = lax.optimization_barrier((far, total))
    beside_far = lax.ppermute(far, "blk", across)
    beside, total = lax.optimization_barrier((beside, total))
    beside_below = lax.ppermute(beside, "blk", upward)
    beside_above = lax.ppermute(beside, "blk", downward)
    total = products(scale, pi, [beside, far, below, above], total, "products_near")
    total = products(scale, pi, [beside_far], total, "products_far")
    total = products(scale, pi, [beside_above], total, "products_above")
    return products(scale, pi, [beside_below], total, "products_last", last=True)


def shards(
    walker_matrix, updates, update_rows, left_table, right_table, assignment, momentum_sum,
    transfer_momentum, transfer_frequency, ownership, g4_prior,
):
    pi = labels(ownership, momentum_sum, transfer_momentum, transfer_frequency)
    greens = walker(walker_matrix[0, 0], updates[0, 0], update_rows[0, 0], left_table, right_table)
    measured = permute_walkers(greens, assignment)
    scale = 1.0 / lax.axis_size("blk")
    return cycle_products(scale, pi, measured, g4_prior[0])[None]


def solution(mesh):
    placed = (
        P("grp", "blk", None, None),
        P("grp", "blk", None, None, None),
        P("grp", "blk", None, None),
        P(),
        P(),
        P("blk", None),
        P(),
        P(),
        P(),
        P("blk"),
        P("grp", "blk", None, None),
    )
    return jax.shard_map(
        shards, mesh=mesh, in_specs=placed, out_specs=P("grp", "blk", None, None), check_vma=False
    )
```

```python
import functools

import jax
import jax.numpy as jnp
from jax import lax
from jax.experimental import pallas as pl
from jax.experimental.pallas import tpu as pltpu
from jax.sharding import PartitionSpec as P

UPD = 4
RANK = 256
ORDER = 1024
NW = 16
NK = 16
KW = 256
M_FIRST = 768
F32 = jnp.float32
BF16 = jnp.bfloat16

HBM = pl.BlockSpec(memory_space=pltpu.HBM)
VMEM = pl.BlockSpec(memory_space=pltpu.VMEM)
SMEM = pl.BlockSpec(memory_space=pltpu.SMEM)


def split(x):
    hi = x.astype(BF16)
    return hi, (x - hi.astype(F32)).astype(BF16)


def mm(a, b):
    return jnp.dot(a, b, preferred_element_type=F32)


def mm_nt(a, b):
    return lax.dot_general(a, b, (((1,), (1,)), ((), ())), preferred_element_type=F32)


def mm_split(hi, lo, b, product=mm):
    count = hi.shape[0]
    both = product(jnp.concatenate([hi, lo]), b)
    return both[:count] + both[count:]


def walker_kernel(m_hbm, u_hbm, rows_hbm, l_hbm, r_hbm, out_ref, m_v, u_v, rows_v, l_v, r_v, p_ref, s_ref, sems):
    copy_rows = pltpu.make_async_copy(rows_hbm, rows_v, sems.at[0])
    copy_l = pltpu.make_async_copy(l_hbm, l_v, sems.at[1])
    copy_r = pltpu.make_async_copy(r_hbm, r_v, sems.at[2])
    copy_u = [pltpu.make_async_copy(u_hbm.at[u], u_v.at[u], sems.at[3 + u]) for u in range(UPD)]
    spans = [pl.ds(0, M_FIRST), pl.ds(M_FIRST, ORDER - M_FIRST)]
    copy_m = [
        pltpu.make_async_copy(m_hbm.at[span, :], m_v.at[span, :], sems.at[3 + UPD + k])
        for k, span in enumerate(spans)
    ]
    for copy in (copy_rows, copy_r, *copy_m, copy_l, copy_u[3], copy_u[2], copy_u[0], copy_u[1]):
        copy.start()

    lane = lax.broadcasted_iota(jnp.int32, (RANK, ORDER), 1)
    copy_rows.wait()
    for u in range(UPD):
        column = jnp.broadcast_to(rows_v[pl.ds(u, 1), :], (128, RANK)).T[:, :1]
        s_ref[u] = jnp.where(lane == column, 1.0, 0.0).astype(BF16)

    copy_r.wait()
    r_hi, r_lo = split(r_v[...].T)

    def multiply(span):
        m_hi, m_lo = split(m_v[span, :])
        p_ref[:, span] = mm_split(r_hi, r_lo, m_hi, mm_nt) + mm_nt(r_hi, m_lo)

    copy_m[0].wait()
    multiply(spans[0])
    for copy in (copy_m[1], copy_l, *copy_u):
        copy.wait()
    left = l_v[...].T
    multiply(spans[1])
    right = p_ref[...]
    for early, late in ((0, 3), (1, 2)):
        right_hi, right_lo = split(right)
        x_hi, x_lo = split(mm_split(right_hi, right_lo, s_ref[early], mm_nt))
        right = right + mm_split(x_hi, x_lo, u_v[early], mm_nt)
        left_hi, left_lo = split(left)
        x_hi, x_lo = split(mm_split(left_hi, left_lo, u_v[late]))
        left = left + mm_split(x_hi, x_lo, s_ref[late])
    left_hi, left_lo = split(left)
    right_hi, right_lo = split(right)
    out_ref[...] = mm_split(left_hi, left_lo, right_hi, mm_nt) + mm_nt(left_hi, right_lo)


def walker(matrix, updates, rows, left, right):
    return pl.pallas_call(
        walker_kernel,
        out_shape=jax.ShapeDtypeStruct((KW, KW), F32),
        in_specs=[HBM] * 5,
        out_specs=VMEM,
        scratch_shapes=[
            pltpu.VMEM((ORDER, ORDER), F32),
            pltpu.VMEM((UPD, ORDER, RANK), BF16),
            pltpu.VMEM((UPD, RANK), jnp.int32),
            pltpu.VMEM((ORDER, KW), F32),
            pltpu.VMEM((ORDER, KW), F32),
            pltpu.VMEM((KW, ORDER), F32),
            pltpu.VMEM((UPD, RANK, ORDER), BF16),
            pltpu.SemaphoreType.DMA((5 + UPD,)),
        ],
        compiler_params=pltpu.CompilerParams(vmem_limit_bytes=24 << 20),
        name="walker",
    )(*(pltpu.with_memory_space_constraint(x, pltpu.HBM) for x in (matrix, updates, rows, left, right)))


def route_kernel(core_ref, targets_ref, own_ref, other_ref, out_ref):
    core = core_ref[0]
    for pair in range(own_ref.shape[0]):
        for part, source_ref in ((core, own_ref), (1 - core, other_ref)):
            target = targets_ref[0, 2 * pair + part]

            @pl.when((target & 1) == core)
            def _():
                out_ref[target >> 1] = source_ref[pair]


def route(core, targets, own, other):
    return pl.pallas_call(
        route_kernel,
        out_shape=jax.ShapeDtypeStruct(own.shape, F32),
        in_specs=[SMEM, SMEM, VMEM, VMEM],
        out_specs=VMEM,
        compiler_params=pltpu.CompilerParams(vmem_limit_bytes=8 << 20),
        name="route",
    )(core, targets, own, other)


def permute_walkers(greens, targets, pi):
    n_grp = lax.axis_size("grp")
    pairs = n_grp // 2
    core = lax.axis_index("grp") & 1
    alike = [[2 * pair + part for pair in range(pairs)] for part in range(2)]
    chunks = greens.reshape(pairs, KW // pairs, KW)
    own = lax.all_to_all(chunks, "grp", 0, 0, axis_index_groups=alike, tiled=True)
    other = lax.ppermute(own, "grp", [(w, w ^ 1) for w in range(n_grp)])
    other, pi = lax.optimization_barrier((other, pi))
    routed = route(core.reshape(1), targets, own, other)
    return lax.all_to_all(routed, "grp", 0, 0, axis_index_groups=alike, tiled=True).reshape(KW, KW), pi


def labels_kernel(own_ref, ms_ref, tm_ref, tf_ref, pi_ref):
    lanes = lax.broadcasted_iota(jnp.int32, (NW, KW), 1)
    steps = lax.broadcasted_iota(jnp.int32, (NW, KW), 0)
    for j in range(own_ref.shape[0]):
        label = own_ref[j]
        moment = tm_ref[label]
        spot = (steps + tf_ref[label]) % NW
        for kappa in range(NK):
            goal = spot + ms_ref[kappa, moment] * NW
            pi_ref[pl.ds(j * KW + kappa * NW, NW), :] = jnp.where(lanes == goal, 1.0, 0.0).astype(BF16)


def labels(ownership, momentum_sum, moments, freqs):
    held = ownership.shape[0]
    return pl.pallas_call(
        labels_kernel,
        out_shape=jax.ShapeDtypeStruct((held * KW, KW), BF16),
        in_specs=[SMEM] * 4,
        out_specs=VMEM,
        cost_estimate=pl.CostEstimate(flops=4_000_000, bytes_accessed=1_000_000, transcendentals=0),
        compiler_params=pltpu.CompilerParams(vmem_limit_bytes=8 << 20),
        name="labels",
    )(ownership, momentum_sum, moments, freqs)


def products_kernel(scale, last, pi_ref, *refs):
    if last:
        *piece_refs, total_ref, out_hbm, out_v, sems = refs
    else:
        *piece_refs, total_ref, out_ref = refs
    held = total_ref.shape[0]
    pi = pi_ref[...]
    blocks = []
    for piece_ref in piece_refs:
        a_hi, a_lo = split(piece_ref[...])
        blocks.append((mm_nt(pi, a_hi).astype(BF16), mm_nt(pi, a_lo).astype(BF16)))
    for j in range(held):
        rows = slice(j * KW, (j + 1) * KW)
        term = total_ref[j]
        for piece_ref, (v_hi, v_lo) in zip(piece_refs, blocks):
            term += piece_ref[...] * scale * (mm_nt(v_hi[rows], pi[rows]) + mm_nt(v_lo[rows], pi[rows]))
        if last:
            out_v[j] = term
            pltpu.make_async_copy(out_v.at[j], out_hbm.at[j], sems.at[j]).start()
        else:
            out_ref[j] = term
    if last:
        for j in range(held):
            pltpu.make_async_copy(out_v.at[j], out_hbm.at[j], sems.at[j]).wait()


def products(scale, pi, pieces, total, name, last=False):
    held = total.shape[0]
    count = len(pieces)
    return pl.pallas_call(
        functools.partial(products_kernel, scale, last),
        out_shape=jax.ShapeDtypeStruct(total.shape, F32),
        in_specs=[VMEM] * (2 + count),
        out_specs=HBM if last else VMEM,
        scratch_shapes=[pltpu.VMEM(total.shape, F32), pltpu.SemaphoreType.DMA((held,))] if last else [],
        cost_estimate=pl.CostEstimate(
            flops=count * held * 8 * KW**3, bytes_accessed=4 * KW * KW * (2 * held + count), transcendentals=0
        ),
        compiler_params=pltpu.CompilerParams(vmem_limit_bytes=16 << 20),
        name=name,
    )(pi, *pieces, total)


def cycle_products(scale, pi, own, prior):
    across = [(j, (j + 4) % 8) for j in range(8)]
    upward = [(j, j // 4 * 4 + (j % 4 + 1) % 4) for j in range(8)]
    downward = [(j, j // 4 * 4 + (j % 4 + 3) % 4) for j in range(8)]
    opposite = [(j, j // 4 * 4 + (j % 4 + 2) % 4) for j in range(8)]
    far = lax.ppermute(own, "blk", opposite)
    beside = lax.ppermute(own, "blk", across)
    below = lax.ppermute(own, "blk", upward)
    above = lax.ppermute(own, "blk", downward)
    total = products(scale, pi, [own], prior, "products_own")
    far, total = lax.optimization_barrier((far, total))
    beside_far = lax.ppermute(far, "blk", across)
    beside, total = lax.optimization_barrier((beside, total))
    beside_below = lax.ppermute(beside, "blk", upward)
    beside_above = lax.ppermute(beside, "blk", downward)
    total = products(scale, pi, [beside, far, below, above], total, "products_near")
    total = products(scale, pi, [beside_far], total, "products_far")
    total = products(scale, pi, [beside_above], total, "products_above")
    return products(scale, pi, [beside_below], total, "products_last", last=True)


def shards(
    walker_matrix, updates, update_rows, left_table, right_table, assignment, momentum_sum,
    transfer_momentum, transfer_frequency, ownership, g4_prior,
):
    pi = labels(ownership, momentum_sum, transfer_momentum, transfer_frequency)
    greens = walker(walker_matrix[0, 0], updates[0, 0], update_rows[0, 0], left_table, right_table)
    measured, pi = permute_walkers(greens, assignment, pi)
    scale = 1.0 / lax.axis_size("blk")
    return cycle_products(scale, pi, measured, g4_prior[0])[None]


def solution(mesh):
    placed = (
        P("grp", "blk", None, None),
        P("grp", "blk", None, None, None),
        P("grp", "blk", None, None),
        P(),
        P(),
        P("blk", None),
        P(),
        P(),
        P(),
        P("blk"),
        P("grp", "blk", None, None),
    )
    return jax.shard_map(
        shards, mesh=mesh, in_specs=placed, out_specs=P("grp", "blk", None, None), check_vma=False
    )
```
